128 devices in a mesh: tins: 16 (over x, y_hi, core), space: 8 (over z, y_lo).
Axes of the slice: x: 4, y: 4 (y_hi: 2, y_lo: 2; y = y_hi * 2 + y_lo), z: 4, core: 2. Of those that a mesh axis runs over, the one named last changes fastest.
Arguments:
- eigvecs: bfloat16 [16, 2, 128, 3, 4096], P('tins', None, None, None, 'space'), may hold values from -6 to 6
- momenta: int32 [1, 3], replicated, may hold values from -2 to 2, as said below
- gamma_table: int32 [2, 4], replicated, may hold values from 0 to 3, as said below
- forward: bfloat16 [16, 2, 512, 128], P('tins'), may hold values from -0.375 to 0.375
- backward: bfloat16 [16, 16, 2, 512, 512], P('tins', None, None, 'space'), may hold values from -0.1875 to 0.1875
Outputs:
- three_point: float32 [16, 1, 2, 512, 128], P('tins', None, None, 'space')
The draws below stay inside these ranges and needn't reach their ends.
Inputs may be any that keep to these rules, and one draw needn't show every extreme that they name: `momenta`: each momentum's first component is nonzero. `gamma_table`: row 0 is a permutation of the 4 spins; row 1 holds powers of i.
All inputs are finite; a program needn't handle non-finite values.
Results may differ from the reference program's by a relative error of at most 0.0049.
Values may be sent and summed in bfloat16 or wider, within the bound.
A program may use at most 64 MiB of HBM per device.

```python
import math
import jax
import jax.numpy as jnp
from jax import lax

NEV = 128
NS = 4
COLORS = 3
LS = 96
NSRC = 128
NMOM = 1
NT = 16
SITES = 4096
SPINEV = 512


def draw_momenta(key, part):
    key_rest = jax.random.fold_in(key, 11)
    key_size = jax.random.fold_in(key, 12)
    key_sign = jax.random.fold_in(key, 13)
    key_lead = jax.random.fold_in(key, 14)
    others = jax.random.randint(key_rest, (NMOM, 3), -2, 3)
    magnitude = jax.random.randint(key_size, (NMOM,), 1, 3)
    signs = 2 * jax.random.randint(key_sign, (NMOM,), 0, 2) - 1
    leading = 2 * jax.random.randint(key_lead, (), 0, 2) - 1
    first_col = magnitude * signs
    first_col = first_col.at[0].set(2 * leading)
    result = others.at[:, 0].set(first_col)
    result = result.at[0, 1].set(-2 * leading)
    return result.astype(jnp.int32)


def draw_gamma_table(key, part):
    key_perm = jax.random.fold_in(key, 21)
    key_power = jax.random.fold_in(key, 22)
    key_spot = jax.random.fold_in(key, 23)
    perm = jax.random.permutation(key_perm, NS).astype(jnp.int32)
    powers = jax.random.randint(key_power, (NS,), 0, 4)
    spot = jax.random.randint(key_spot, (), 0, NS)
    powers = jnp.where(jnp.arange(NS, dtype=jnp.int32) == spot, 3, powers)
    return jnp.stack([perm, powers.astype(jnp.int32)], axis=0)


def block_scale(rng, shape, pieces, smallest, high):
    gain, own = 1.0, jax.random.fold_in(rng, 6)
    for axis_at, parts in pieces:
        steps = jnp.exp(jax.random.uniform(jax.random.fold_in(own, axis_at), (parts,), jnp.float32, smallest / len(pieces), high / len(pieces)))
        gain = gain * jnp.repeat(steps, shape[axis_at] // parts).reshape([-1 if axis == axis_at else 1 for axis in range(len(shape))])
    return gain


def normal_values(rng, dims, spread, most, split=(), held_as=jnp.bfloat16):
    factor_of = block_scale(rng, dims, split, -0.22, 0.18) if split else 1.0
    drawn = jax.random.normal(rng, dims, jnp.float32) * spread * factor_of
    return jnp.minimum(jnp.maximum(drawn, -most), most).astype(held_as)


def setup_inputs(seed: int = 0) -> dict:
    seeds = jax.random.split(jax.random.key(seed), 6)
    return {
        "eigvecs": normal_values(seeds[0], (NT, 2, NEV, COLORS, SITES), 1.0, 6.0, ((0, 16), (4, 8))),
        "momenta": draw_momenta(jax.random.fold_in(seeds[5], 71), 0),
        "gamma_table": draw_gamma_table(jax.random.fold_in(seeds[5], 71), 0),
        "forward": normal_values(seeds[3], (NT, 2, SPINEV, NSRC), (2 * NEV) ** -0.5, 0.375, ((0, 16),)),
        "backward": normal_values(seeds[4], (NT, NT, 2, SPINEV, SPINEV), (2 * SPINEV) ** -0.5, 0.1875, ((0, 16), (3, 8))),
    }


def site_phases(momenta, sites):
    coord_x = sites % LS
    coord_y = sites // LS % LS
    coord_z = sites // (LS * LS)
    turns = (momenta[:, 0:1] * coord_x[None, :] + momenta[:, 1:2] * coord_y[None, :] + momenta[:, 2:3] * coord_z[None, :]) % LS
    angle = 2.0 * math.pi / LS * turns.astype(jnp.float32)
    return (jnp.cos(angle), -jnp.sin(angle))

def spin_tables(gamma_table):
    spins = jnp.arange(NS, dtype=jnp.int32)
    onehot = (gamma_table[0][:, None] == spins[None, :]).astype(jnp.float32)
    powers = gamma_table[1]
    cosine = (powers == 0).astype(jnp.float32) - (powers == 2).astype(jnp.float32)
    sine = (powers == 1).astype(jnp.float32) - (powers == 3).astype(jnp.float32)
    return (onehot * cosine[:, None], onehot * sine[:, None])

def elemental_of(vectors, phase_re, phase_im):
    vec_re = vectors[0].astype(jnp.float32)
    vec_im = vectors[1].astype(jnp.float32)
    wave_re = (phase_re[:, None, None, :] * vec_re[None] - phase_im[:, None, None, :] * vec_im[None]).astype(jnp.bfloat16)
    wave_im = (phase_re[:, None, None, :] * vec_im[None] + phase_im[:, None, None, :] * vec_re[None]).astype(jnp.bfloat16)
    wave_re = lax.optimization_barrier(wave_re).astype(jnp.float32)
    wave_im = lax.optimization_barrier(wave_im).astype(jnp.float32)

    def inner(left, right):
        return jnp.einsum('acs,mbcs->mab', left, right, precision=lax.Precision.HIGHEST)
    elem_re = inner(vec_re, wave_re) + inner(vec_im, wave_im)
    elem_im = inner(vec_re, wave_im) - inner(vec_im, wave_re)
    scale = 1.0 / math.sqrt(3.0 * SITES)
    elem = (jnp.stack([elem_re, elem_im], axis=1) * scale).astype(jnp.bfloat16)
    return lax.optimization_barrier(elem)

def images_of(elem, fwd, coef_re, coef_im):
    moments = elem.shape[0]
    elem32 = elem.astype(jnp.float32)
    fwd32 = fwd.astype(jnp.float32).reshape(2, NS, NEV, fwd.shape[-1])

    def product(left, right):
        return jnp.einsum('mab,sbc->msac', left, right, precision=lax.Precision.HIGHEST)
    grid_re = product(elem32[:, 0], fwd32[0]) - product(elem32[:, 1], fwd32[1])
    grid_im = product(elem32[:, 0], fwd32[1]) + product(elem32[:, 1], fwd32[0])

    def permute(table, grid):
        return jnp.einsum('ts,msac->mtac', table, grid, precision=lax.Precision.HIGHEST)
    image_re = permute(coef_re, grid_re) - permute(coef_im, grid_im)
    image_im = permute(coef_im, grid_re) + permute(coef_re, grid_im)
    image = jnp.stack([image_re, image_im], axis=1).reshape(moments, 2, NS * NEV, fwd.shape[-1])
    return lax.optimization_barrier(image.astype(jnp.bfloat16))

def contract(back_block, image):
    back32 = back_block.astype(jnp.float32)
    image32 = image.astype(jnp.float32)

    def product(left, right):
        return jnp.einsum('ij,mjc->mic', left, right, precision=lax.Precision.HIGHEST)
    out_re = product(back32[0], image32[:, 0]) - product(back32[1], image32[:, 1])
    out_im = product(back32[0], image32[:, 1]) + product(back32[1], image32[:, 0])
    return jnp.stack([out_re, out_im], axis=1)

def reference(eigvecs, momenta, gamma_table, forward, backward):
    phase_re, phase_im = site_phases(momenta, jnp.arange(SITES, dtype=jnp.int32))
    coef_re, coef_im = spin_tables(gamma_table)

    def per_time(inputs):
        vectors, fwd = inputs
        elem = elemental_of(vectors.reshape(2, NEV, COLORS, SITES), phase_re, phase_im)
        return images_of(elem, fwd, coef_re, coef_im)
    images_all = lax.map(per_time, (eigvecs, forward))

    def per_sink(back_row):

        def step(totals, item):
            back_block, image = item
            return (totals + contract(back_block, image), None)
        initial = jnp.zeros((NMOM, 2, NS * NEV, NSRC), jnp.float32)
        totals, _ = lax.scan(step, initial, (back_row, images_all))
        return totals * (1.0 / math.sqrt(NT))
    return lax.map(per_sink, backward)
```

```python
import functools
import math

import jax
import jax.numpy as jnp
from jax import lax
from jax.experimental import pallas as pl
from jax.experimental.pallas import tpu as pltpu
from jax.sharding import PartitionSpec as P

MESH = pl.DeviceIdType.MESH
F32 = jnp.float32
BF16 = jnp.bfloat16
NEV, NS, COLORS, LS, NSRC, NT, SPACE = 128, 4, 3, 96, 128, 16, 8
SITES_TOTAL = 4096
SITES = SITES_TOTAL // SPACE
SLICE = NEV // SPACE
ORDERS = (("z", "y", "x"), ("y", "x", "z"), ("x", "z", "y"))
UNITS = ((0, 3), (3, 3), (6, 2))


def site_phases(mom_ref, space):
    site = (space * SITES + lax.broadcasted_iota(jnp.int32, (1, SITES), 1)).astype(F32)
    line = jnp.floor((site + 0.5) * (1.0 / LS))
    coord_x = site - LS * line
    coord_z = jnp.floor((line + 0.5) * (1.0 / LS))
    coord_y = line - LS * coord_z
    m = [mom_ref[0, i].astype(F32) for i in range(3)]
    turns = m[0] * coord_x + m[1] * coord_y + m[2] * coord_z
    turns = turns - LS * jnp.floor((turns + 0.5) * (1.0 / LS))
    angle = (2.0 * math.pi / LS) * turns
    return jnp.cos(angle), -jnp.sin(angle)


def kernel(
    mom_ref, gam_ref, eig_hbm, fwd_hbm, back_hbm, out_ref,
    eig, fwd, bbuf, part, rs, wgt, img0, img1, img2, fin, finr,
    load_sem, swap_sem, rs_send, rs_recv, s1, r1, s2, r2, s3, r3, s4, r4, fin_sem,
):
    t = lax.axis_index("tins")
    space = lax.axis_index("space")
    core = lax.rem(t, 2)
    me = {
        "x": lax.div(t, 4),
        "y": lax.rem(lax.div(t, 2), 2) * 2 + lax.rem(space, 2),
        "z": lax.div(space, 2),
    }
    partner = (t + 1 - 2 * core, space)

    def step(v, d):
        return lax.rem(v + (d + 4) % 4, 4) if d % 4 else v

    def neighbour(axis, d):
        at = dict(me)
        at[axis] = step(me[axis], d)
        return (
            at["x"] * 4 + lax.div(at["y"], 2) * 2 + core,
            at["z"] * 2 + lax.rem(at["y"], 2),
        )

    loads = [
        pltpu.make_async_copy(eig_hbm, eig, load_sem.at[0]),
        pltpu.make_async_copy(fwd_hbm, fwd, load_sem.at[1]),
        pltpu.make_async_copy(back_hbm.at[:, core], bbuf.at[:, core], load_sem.at[2]),
    ]
    for load in loads:
        load.start()

    barrier = pltpu.get_barrier_semaphore()
    peers = [partner]
    peers += [(t, lax.rem(space + d, SPACE)) for d in range(1, SPACE)]
    peers += [neighbour("x", d) for d in (1, -1, 2)]
    peers += [neighbour("y", 2)]
    across = lax.rem(me["y"] + 3 + 2 * lax.rem(me["y"], 2), 4)
    peers += [(me["x"] * 4 + lax.div(across, 2) * 2 + core, me["z"] * 2 + lax.rem(across, 2))]
    for peer in peers:
        pl.semaphore_signal(barrier, inc=1, device_id=peer, device_id_type=MESH)

    phase_re, phase_im = site_phases(mom_ref, space)
    loads[0].wait()
    total = jnp.zeros((NEV, 2 * NEV), F32)
    nt = (((1,), (1,)), ((), ()))
    for color in range(COLORS):
        vec_re = eig[0, color]
        vec_im = eig[1, color]
        wide_re, wide_im = vec_re.astype(F32), vec_im.astype(F32)
        wave_re = (phase_re * wide_re - phase_im * wide_im).astype(BF16)
        wave_im = (phase_re * wide_im + phase_im * wide_re).astype(BF16)
        right = jnp.concatenate([wave_re, wave_im], axis=0)
        total += lax.dot_general(vec_re, right, nt, preferred_element_type=F32)
        right = jnp.concatenate([wave_im, -wave_re], axis=0)
        total += lax.dot_general(vec_im, right, nt, preferred_element_type=F32)
    part[...] = total.reshape(SPACE, SLICE, 2 * NEV)

    pl.semaphore_wait(barrier, len(peers))
    copies = []

    def send(src, dst, send_sem, recv_sem, device):
        copy = pltpu.make_async_remote_copy(
            src_ref=src, dst_ref=dst, send_sem=send_sem, recv_sem=recv_sem,
            device_id=device, device_id_type=MESH,
        )
        copy.start()
        copies.append(copy)
        return copy

    scatter = []
    for d in range(1, SPACE):
        to = lax.rem(space + d, SPACE)
        scatter.append(send(part.at[to], rs.at[d], rs_send.at[d], rs_recv.at[d], (t, to)))
    swap = send(
        back_hbm.at[:, 1 - core], bbuf.at[:, core], swap_sem.at[0], swap_sem.at[1], partner
    )

    loads[1].wait()
    for spin in range(NS):
        source = gam_ref[0, spin]
        power = gam_ref[1, spin]
        cosine = jnp.where(power == 0, 1.0, 0.0) - jnp.where(power == 2, 1.0, 0.0)
        sine = jnp.where(power == 1, 1.0, 0.0) - jnp.where(power == 3, 1.0, 0.0)
        fwd_re = fwd[0, source].astype(F32)
        fwd_im = fwd[1, source].astype(F32)
        rot_re = (cosine * fwd_re - sine * fwd_im).astype(BF16)
        rot_im = (sine * fwd_re + cosine * fwd_im).astype(BF16)
        at = spin * 2 * NSRC
        wgt[0:NEV, at : at + NSRC] = rot_re
        wgt[0:NEV, at + NSRC : at + 2 * NSRC] = rot_im
        wgt[NEV:, at : at + NSRC] = -rot_im
        wgt[NEV:, at + NSRC : at + 2 * NSRC] = rot_re

    elem = part[space]
    for d in range(1, SPACE):
        scatter[d - 1].wait_recv()
        elem += rs[d]
    elem = (elem * (1.0 / math.sqrt(3.0 * SITES_TOTAL))).astype(BF16)
    image = jnp.dot(elem, wgt[...], preferred_element_type=F32).astype(BF16)

    imgs = (img0, img1, img2)
    for j, (a, b, c) in enumerate(ORDERS):
        first, count = UNITS[j]
        for i in range(count):
            at = (first + i) * NSRC
            imgs[j][me[c], me[b], me[a], i] = image[:, at : at + NSRC]

    def line(j, dc, db, half=None):
        _, b, c = ORDERS[j]
        ref = imgs[j].at[step(me[c], dc), step(me[b], db)]
        return ref if half is None else ref.at[pl.ds(half * 2, 2)]

    got1 = {}
    for j, (a, b, c) in enumerate(ORDERS):
        own = imgs[j].at[me[c], me[b], me[a]]
        for i, d in enumerate((1, -1, 2)):
            got1[j, i] = send(own, own, s1.at[j, i], r1.at[j, i], neighbour(a, d))
    got2, got3, got4 = {}, {}, {}

    def pass_line(j, n, db):
        c = ORDERS[j][2]
        for i, d in enumerate((1, -1)):
            got3[j, n, i] = send(
                line(j, 0, db), line(j, 0, db), s3.at[j, n, i], r3.at[j, n, i], neighbour(c, d)
            )

    def pass_on(j, n, db, i):
        d = (1, -1)[i]
        got3[j, n, i].wait_recv()
        from_plane = line(j, -d, db)
        got4[j, n] = send(
            from_plane, from_plane, s4.at[j, n], r4.at[j, n], neighbour(ORDERS[j][2], d)
        )

    for j in range(3):
        for i in range(3):
            got1[j, i].wait_recv()
        for i, d in enumerate((1, -1)):
            got2[j, i] = send(
                line(j, 0, 0), line(j, 0, 0), s2.at[j, i], r2.at[j, i], neighbour(ORDERS[j][1], d)
            )
    for j in range(3):
        pass_line(j, 0, 0)
    for i, d in enumerate((1, -1)):
        for j in range(3):
            got2[j, i].wait_recv()
            half = line(j, 0, -d, i)
            got2[j, 2 + i] = send(
                half, half, s2.at[j, 2 + i], r2.at[j, 2 + i], neighbour(ORDERS[j][1], d)
            )
            pass_line(j, 1 + i, -d)
    for j in range(3):
        pass_on(j, 0, 0, 0)
    for j in range(3):
        got2[j, 2].wait_recv()
        got2[j, 3].wait_recv()
        pass_line(j, 3, 2)
    for j in range(3):
        pass_on(j, 1, -1, 1)
    for j in range(3):
        pass_on(j, 2, 1, 1)
    for j in range(3):
        pass_on(j, 3, 2, 0)
    for j in range(3):
        for n, i in ((0, 1), (1, 0), (2, 0), (3, 1)):
            got3[j, n, i].wait_recv()
        for n in range(4):
            got4[j, n].wait_recv()

    loads[2].wait()
    swap.wait_recv()
    acc = jnp.zeros((4 * 64, 2 * NSRC), F32)
    for k in range(NT // 2):
        x, y_hi = k // 2, k % 2
        rows = []
        for spin in range(NS):
            halves = []
            for half in range(2):
                unit = spin * 2 + half
                j = 0 if unit < 3 else (1 if unit < 6 else 2)
                tiles = []
                for s in range(SPACE):
                    at = {"x": x, "y": y_hi * 2 + s % 2, "z": s // 2}
                    a, b, c = ORDERS[j]
                    tiles.append(imgs[j][at[c], at[b], at[a], unit - UNITS[j][0]])
                halves.append(jnp.concatenate(tiles, axis=0))
            rows.append(jnp.concatenate(halves, axis=1))
        right = jnp.concatenate(rows, axis=0)
        left = bbuf[k].reshape(4 * 64, NS * NEV)
        acc += jnp.dot(left, right, preferred_element_type=F32)
    for u in range(2):
        top = acc[u * 128 : u * 128 + 64]
        low = acc[u * 128 + 64 : u * 128 + 128]
        fin[u, 0] = top[:, :NSRC] - low[:, NSRC:]
        fin[u, 1] = top[:, NSRC:] + low[:, :NSRC]
    last = send(fin.at[1 - core], finr, fin_sem.at[0], fin_sem.at[1], partner)
    last.wait_recv()
    out_ref[...] = (fin[core] + finr[...]) * (1.0 / math.sqrt(NT))
    for copy in copies:
        copy.wait_send()


def on_device(eigvecs, momenta, gamma_table, forward, backward):
    eig = eigvecs[0].transpose(0, 2, 1, 3)
    fwd = forward.reshape(2, NS, NEV, NSRC)
    back = backward.reshape(NT // 2, 2, 128, NS * NEV)
    dma = pltpu.SemaphoreType.DMA
    out = pl.pallas_call(
        kernel,
        name="three_point",
        out_shape=jax.ShapeDtypeStruct((2, 64, NSRC), F32),
        in_specs=[pl.BlockSpec(memory_space=pltpu.SMEM)] * 2
        + [pl.BlockSpec(memory_space=pl.ANY)] * 3,
        out_specs=pl.BlockSpec(memory_space=pltpu.VMEM),
        scratch_shapes=[
            pltpu.VMEM((2, COLORS, NEV, SITES), BF16),
            pltpu.VMEM((2, NS, NEV, NSRC), BF16),
            pltpu.VMEM((NT // 2, 2, 128, NS * NEV), BF16),
            pltpu.VMEM((SPACE, SLICE, 2 * NEV), F32),
            pltpu.VMEM((SPACE, SLICE, 2 * NEV), F32),
            pltpu.VMEM((2 * NEV, NS * 2 * NSRC), BF16),
            *[pltpu.VMEM((4, 4, 4, count, SLICE, NSRC), BF16) for _, count in UNITS],
            pltpu.VMEM((2, 2, 64, NSRC), F32),
            pltpu.VMEM((2, 64, NSRC), F32),
            dma((3,)), dma((2,)), dma((SPACE,)), dma((SPACE,)),
            dma((3, 3)), dma((3, 3)), dma((3, 4)), dma((3, 4)),
            dma((3, 4, 2)), dma((3, 4, 2)), dma((3, 4)), dma((3, 4)), dma((2,)),
        ],
        compiler_params=pltpu.CompilerParams(collective_id=0, has_side_effects=True),
    )(momenta, gamma_table, eig, fwd, back)
    return out[None, None]


def solution(mesh):
    placed = (
        P("tins", None, None, None, "space"),
        P(),
        P(),
        P("tins", None, None, None),
        P("tins", None, None, "space", None),
    )
    return jax.shard_map(
        on_device,
        mesh=mesh,
        in_specs=placed,
        out_specs=P("tins", None, None, "space", None),
        check_vma=False,
    )
```

```python
import functools
import math

import jax
import jax.numpy as jnp
from jax import lax
from jax.experimental import pallas as pl
from jax.experimental.pallas import tpu as pltpu
from jax.sharding import PartitionSpec as P

MESH = pl.DeviceIdType.MESH
F32 = jnp.float32
BF16 = jnp.bfloat16
NEV, NS, COLORS, LS, NSRC, NT, SPACE = 128, 4, 3, 96, 128, 16, 8
SITES_TOTAL = 4096
SITES = SITES_TOTAL // SPACE
SLICE = NEV // SPACE
ROWS_X, ROWS_Y, ROWS_Z = pl.ds(0, 32), pl.ds(32, 32), pl.ds(64, 64)
SHIFTS = (1, -1, 2)


def site_phases(mom_ref, space):
    site = (space * SITES + lax.broadcasted_iota(jnp.int32, (1, SITES), 1)).astype(F32)
    line = jnp.floor((site + 0.5) * (1.0 / LS))
    coord_x = site - LS * line
    coord_z = jnp.floor((line + 0.5) * (1.0 / LS))
    coord_y = line - LS * coord_z
    m = [mom_ref[0, i].astype(F32) for i in range(3)]
    turns = m[0] * coord_x + m[1] * coord_y + m[2] * coord_z
    turns = turns - LS * jnp.floor((turns + 0.5) * (1.0 / LS))
    angle = (2.0 * math.pi / LS) * turns
    return jnp.cos(angle), -jnp.sin(angle)


def kernel(
    mom_ref, gam_ref, eig_hbm, fwd_hbm, back_hbm, out_ref,
    eig, fbuf, bbuf, part, rs, ebuf, gbuf, fin, finr,
    load_sem, swap_sem, rs_send, rs_recv, e_send, e_recv, f_send, f_recv, fin_sem,
):
    t = lax.axis_index("tins")
    space = lax.axis_index("space")
    core = lax.rem(t, 2)
    x, y_hi = lax.div(t, 4), lax.rem(lax.div(t, 2), 2)
    z, y_lo = lax.div(space, 2), lax.rem(space, 2)
    k_own = lax.div(t, 2)
    partner = (t + 1 - 2 * core, space)

    def step(v, d):
        return lax.rem(v + (d + 4) % 4, 4) if d % 4 else v

    def chip(dx, flip_hi, dz, flip_lo):
        hi = 1 - y_hi if flip_hi else y_hi
        lo = 1 - y_lo if flip_lo else y_lo
        return (step(x, dx) * 4 + hi * 2 + core, step(z, dz) * 2 + lo)

    PAIR, ACROSS, TWO = (False, True), (True, True), (True, False)

    loads = [pltpu.make_async_copy(eig_hbm.at[:, c], eig.at[:, c], load_sem.at[c]) for c in range(COLORS)]
    loads += [
        pltpu.make_async_copy(fwd_hbm, fbuf.at[x, y_hi], load_sem.at[3]),
        pltpu.make_async_copy(back_hbm.at[:, core], bbuf.at[:, core], load_sem.at[4]),
    ]
    for load in loads:
        load.start()

    barrier = pltpu.get_barrier_semaphore()
    peers = [partner]
    peers += [(t, lax.rem(space + d, SPACE)) for d in range(1, SPACE)]
    peers += [chip(d, False, 0, False) for d in SHIFTS]
    peers += [chip(d, True, 0, True) for d in (0, *SHIFTS)]
    peers += [chip(0, True, 0, False)]
    for peer in peers:
        pl.semaphore_signal(barrier, inc=1, device_id=peer, device_id_type=MESH)

    phase_re, phase_im = site_phases(mom_ref, space)
    total = jnp.zeros((NEV, 2 * NEV), F32)
    nt = (((1,), (1,)), ((), ()))
    for color in range(COLORS):
        loads[color].wait()
        vec_re = eig[0, color]
        vec_im = eig[1, color]
        wide_re, wide_im = vec_re.astype(F32), vec_im.astype(F32)
        wave_re = (phase_re * wide_re - phase_im * wide_im).astype(BF16)
        wave_im = (phase_re * wide_im + phase_im * wide_re).astype(BF16)
        right = jnp.concatenate([wave_re, wave_im], axis=0)
        total += lax.dot_general(vec_re, right, nt, preferred_element_type=F32)
        right = jnp.concatenate([wave_im, -wave_re], axis=0)
        total += lax.dot_general(vec_im, right, nt, preferred_element_type=F32)
    part[...] = total.reshape(SPACE, SLICE, 2 * NEV)

    loads[3].wait()
    pl.semaphore_wait(barrier, len(peers))
    copies = []

    def send(src, dst, send_sem, recv_sem, device):
        copy = pltpu.make_async_remote_copy(
            src_ref=src, dst_ref=dst, send_sem=send_sem, recv_sem=recv_sem,
            device_id=device, device_id_type=MESH,
        )
        copy.start()
        copies.append(copy)
        return copy

    scatter = []
    for d in range(1, SPACE):
        to = lax.rem(space + d, SPACE)
        scatter.append(send(part.at[to], rs.at[d], rs_send.at[d], rs_recv.at[d], (t, to)))

    got = {}

    def share(name, block, device):
        n = len(got)
        got[name] = send(block, block, f_send.at[n], f_recv.at[n], device)

    def z_block(dx, flip):
        hi = 1 - y_hi if flip else y_hi
        return fbuf.at[step(x, dx), hi, z, :, ROWS_Z]

    def y_block(dx):
        return fbuf.at[step(x, dx), y_hi, :, y_lo, ROWS_Y]

    def x_block(flip):
        hi = 1 - y_hi if flip else y_hi
        return fbuf.at[x, hi, :, :, ROWS_X]

    for d in (2, 1, -1):
        share(("z1", d, True), z_block(0, False), chip(d, True, 0, True))
        share(("z1", d, False), z_block(0, False), chip(d, False, 0, False))
        share(("y1", d), y_block(0), chip(d, False, 0, False))
    share(("z1", 0, True), z_block(0, False), chip(0, True, 0, True))
    share(("x1",), x_block(False), chip(0, True, 0, True))
    for d in SHIFTS:
        share(("x2", d, False), x_block(False), chip(d, False, 0, False))
    for name, flips in (("across", ACROSS), ("two", TWO)):
        share(("y2", name, 0), y_block(0), chip(0, flips[0], 0, flips[1]))
    swap = send(
        back_hbm.at[:, 1 - core], bbuf.at[:, core], swap_sem.at[0], swap_sem.at[1], partner
    )

    elem = part[space]
    for d in range(1, SPACE):
        scatter[d - 1].wait_recv()
        elem += rs[d]
    own = k_own * SPACE + space
    ebuf[own] = (elem * (1.0 / math.sqrt(3.0 * SITES_TOTAL))).astype(BF16)
    away = [
        (dx, flip_hi, dz, flip_lo)
        for dx in (0, *SHIFTS) for flip_hi in (False, True)
        for dz in (0, *SHIFTS) for flip_lo in (False, True)
    ]
    def hops(at):
        dx, flip_hi, dz, flip_lo = at
        return abs(dx) + abs(dz) + (1 if flip_lo else 2 * flip_hi)
    for at in sorted(away[1:], key=hops, reverse=True):
        pltpu.make_async_remote_copy(
            src_ref=ebuf.at[own], dst_ref=ebuf.at[own], send_sem=e_send.at[0],
            recv_sem=e_recv.at[k_own], device_id=chip(*at), device_id_type=MESH,
        ).start()

    got["x1",].wait_recv()
    for d in SHIFTS:
        share(("x2", d, True), x_block(True), chip(d, False, 0, False))
    for d in SHIFTS:
        got["y1", d].wait_recv()
        for name, flips in (("two", TWO), ("across", ACROSS), ("pair", PAIR)):
            share(("y2", name, d), y_block(-d), chip(0, flips[0], 0, flips[1]))
    for dx, flip in [(0, True)] + [(d, f) for d in SHIFTS for f in (False, True)]:
        got["z1", dx, flip].wait_recv()
        for d in (2, 1, -1):
            share(("z2", dx, flip, d), z_block(-dx, flip), chip(0, False, d, False))

    loads[4].wait()
    swap.wait_recv()
    for spin in range(NS):
        power = gam_ref[1, spin]
        cosine = jnp.where(power == 0, 1.0, 0.0) - jnp.where(power == 2, 1.0, 0.0)
        sine = jnp.where(power == 1, 1.0, 0.0) - jnp.where(power == 3, 1.0, 0.0)
        lanes = pl.ds(spin * NEV, NEV)

        def turn(k, carry):
            for u in range(2):
                back_re = bbuf[k, u, 0:64, lanes].astype(F32)
                back_im = bbuf[k, u, 64:128, lanes].astype(F32)
                bbuf[k, u, 0:64, lanes] = (cosine * back_re - sine * back_im).astype(BF16)
                bbuf[k, u, 64:128, lanes] = (sine * back_re + cosine * back_im).astype(BF16)
            return carry

        lax.fori_loop(0, NT // 2, turn, 0)

    acc = jnp.zeros((4 * 64, 2 * NSRC), F32)
    for dx in (0, *SHIFTS):
        for flip in (False, True):
            x_at, hi_at = step(x, -dx), 1 - y_hi if flip else y_hi
            k = x_at * 2 + hi_at
            here = dx == 0 and not flip
            rows = pl.ds(k * SPACE, SPACE)
            count = pl.ds(0, SPACE - 1) if here else pl.ds(0, SPACE)
            pltpu.make_async_copy(ebuf.at[count], ebuf.at[count], e_recv.at[k]).wait()
            if not here:
                if dx:
                    got["x2", dx, flip].wait_recv()
                if flip:
                    got["y2", "across", dx].wait_recv()
                    got["y2", "two", dx].wait_recv()
                else:
                    got["y2", "pair", dx].wait_recv()
                for d in SHIFTS:
                    got["z2", dx, flip, d].wait_recv()
            elem = ebuf[rows].reshape(NEV, 2 * NEV)
            for spin in range(NS):
                fwd_re = fbuf[x_at, hi_at, spin // 2, spin % 2]
                fwd_im = fbuf[x_at, hi_at, 2 + spin // 2, spin % 2]
                right = jnp.concatenate([
                    jnp.concatenate([fwd_re, fwd_im], axis=1),
                    jnp.concatenate([-fwd_im, fwd_re], axis=1),
                ], axis=0)
                gbuf[spin] = jnp.dot(elem, right, preferred_element_type=F32).astype(BF16)
            image = jnp.concatenate([gbuf[gam_ref[0, spin]] for spin in range(NS)], axis=0)
            left = bbuf[k].reshape(4 * 64, NS * NEV)
            acc += jnp.dot(left, image, preferred_element_type=F32)
    for u in range(2):
        top = acc[u * 128 : u * 128 + 64]
        low = acc[u * 128 + 64 : u * 128 + 128]
        fin[u, 0] = top[:, :NSRC] - low[:, NSRC:]
        fin[u, 1] = top[:, NSRC:] + low[:, :NSRC]
    last = send(fin.at[1 - core], finr, fin_sem.at[0], fin_sem.at[1], partner)
    last.wait_recv()
    out_ref[...] = (fin[core] + finr[...]) * (1.0 / math.sqrt(NT))
    for copy in copies:
        copy.wait_send()
    sent = pl.ds(0, 63)
    pltpu.make_async_copy(ebuf.at[sent], ebuf.at[sent], e_send.at[0]).wait()


def on_device(eigvecs, momenta, gamma_table, forward, backward):
    eig = eigvecs[0].transpose(0, 2, 1, 3)
    fwd = forward.reshape(4, 2, NEV, NSRC)
    back = backward.reshape(NT // 2, 2, 128, NS * NEV)
    dma = pltpu.SemaphoreType.DMA
    out = pl.pallas_call(
        kernel,
        name="three_point",
        out_shape=jax.ShapeDtypeStruct((2, 64, NSRC), F32),
        in_specs=[pl.BlockSpec(memory_space=pltpu.SMEM)] * 2
        + [pl.BlockSpec(memory_space=pl.ANY)] * 3,
        out_specs=pl.BlockSpec(memory_space=pltpu.VMEM),
        scratch_shapes=[
            pltpu.VMEM((2, COLORS, NEV, SITES), BF16),
            pltpu.VMEM((4, 2, 4, 2, NEV, NSRC), BF16),
            pltpu.VMEM((NT // 2, 2, 128, NS * NEV), BF16),
            pltpu.VMEM((SPACE, SLICE, 2 * NEV), F32),
            pltpu.VMEM((SPACE, SLICE, 2 * NEV), F32),
            pltpu.VMEM((64, SLICE, 2 * NEV), BF16),
            pltpu.VMEM((NS, NEV, 2 * NSRC), BF16),
            pltpu.VMEM((2, 2, 64, NSRC), F32),
            pltpu.VMEM((2, 64, NSRC), F32),
            dma((5,)), dma((2,)), dma((SPACE,)), dma((SPACE,)),
            dma((1,)), dma((8,)), dma((49,)), dma((49,)), dma((2,)),
        ],
        compiler_params=pltpu.CompilerParams(collective_id=0, has_side_effects=True),
    )(momenta, gamma_table, eig, fwd, back)
    return out[None, None]


def solution(mesh):
    placed = (
        P("tins", None, None, None, "space"),
        P(),
        P(),
        P("tins", None, None, None),
        P("tins", None, None, "space", None),
    )
    return jax.shard_map(
        on_device,
        mesh=mesh,
        in_specs=placed,
        out_specs=P("tins", None, None, "space", None),
        check_vma=False,
    )
```

```python
import functools
import math

import jax
import jax.numpy as jnp
from jax import lax
from jax.experimental import pallas as pl
from jax.experimental.pallas import tpu as pltpu
from jax.sharding import PartitionSpec as P

MESH = pl.DeviceIdType.MESH
F32 = jnp.float32
BF16 = jnp.bfloat16
NEV, NS, COLORS, LS, NSRC, NT, SPACE = 128, 4, 3, 96, 128, 16, 8
SITES_TOTAL = 4096
SITES = SITES_TOTAL // SPACE
SLICE = NEV // SPACE
ROWS_X, ROWS_Y, ROWS_Z = pl.ds(0, 48), pl.ds(48, 48), pl.ds(96, 32)
SHIFTS = (1, -1, 2)


def site_phases(mom_ref, space):
    site = (space * SITES + lax.broadcasted_iota(jnp.int32, (1, SITES), 1)).astype(F32)
    line = jnp.floor((site + 0.5) * (1.0 / LS))
    coord_x = site - LS * line
    coord_z = jnp.floor((line + 0.5) * (1.0 / LS))
    coord_y = line - LS * coord_z
    m = [mom_ref[0, i].astype(F32) for i in range(3)]
    turns = m[0] * coord_x + m[1] * coord_y + m[2] * coord_z
    turns = turns - LS * jnp.floor((turns + 0.5) * (1.0 / LS))
    angle = (2.0 * math.pi / LS) * turns
    return jnp.cos(angle), -jnp.sin(angle)


def kernel(
    mom_ref, gam_ref, eig_hbm, fwd_hbm, back_hbm, out_ref,
    eig, fbuf, bbuf, part, rs, ebuf, gbuf, fin, finr,
    load_sem, swap_sem, rs_send, rs_recv, e_send, e_recv, f_send, f_recv, fin_sem,
):
    t = lax.axis_index("tins")
    space = lax.axis_index("space")
    core = lax.rem(t, 2)
    x, y_hi = lax.div(t, 4), lax.rem(lax.div(t, 2), 2)
    z, y_lo = lax.div(space, 2), lax.rem(space, 2)
    k_own = lax.div(t, 2)
    partner = (t + 1 - 2 * core, space)

    def step(v, d):
        return lax.rem(v + (d + 4) % 4, 4) if d % 4 else v

    def chip(dx, flip_hi, dz, flip_lo):
        hi = 1 - y_hi if flip_hi else y_hi
        lo = 1 - y_lo if flip_lo else y_lo
        return (step(x, dx) * 4 + hi * 2 + core, step(z, dz) * 2 + lo)

    PAIR, ACROSS, TWO = (False, True), (True, True), (True, False)

    loads = [pltpu.make_async_copy(eig_hbm.at[:, c], eig.at[:, c], load_sem.at[c]) for c in range(COLORS)]
    loads += [
        pltpu.make_async_copy(fwd_hbm, fbuf.at[x, y_hi], load_sem.at[3]),
        pltpu.make_async_copy(back_hbm.at[:, core], bbuf.at[:, core], load_sem.at[4]),
    ]
    for load in loads:
        load.start()

    barrier = pltpu.get_barrier_semaphore()
    peers = [partner]
    peers += [(t, lax.rem(space + d, SPACE)) for d in range(1, SPACE)]
    peers += [chip(d, False, 0, False) for d in SHIFTS]
    peers += [chip(d, True, 0, True) for d in (0, *SHIFTS)]
    peers += [chip(0, True, 0, False)]
    for peer in peers:
        pl.semaphore_signal(barrier, inc=1, device_id=peer, device_id_type=MESH)

    phase_re, phase_im = site_phases(mom_ref, space)
    total = jnp.zeros((NEV, 2 * NEV), F32)
    nt = (((1,), (1,)), ((), ()))
    for color in range(COLORS):
        loads[color].wait()
        vec_re = eig[0, color]
        vec_im = eig[1, color]
        wide_re, wide_im = vec_re.astype(F32), vec_im.astype(F32)
        wave_re = (phase_re * wide_re - phase_im * wide_im).astype(BF16)
        wave_im = (phase_re * wide_im + phase_im * wide_re).astype(BF16)
        right = jnp.concatenate([wave_re, wave_im], axis=0)
        total += lax.dot_general(vec_re, right, nt, preferred_element_type=F32)
        right = jnp.concatenate([wave_im, -wave_re], axis=0)
        total += lax.dot_general(vec_im, right, nt, preferred_element_type=F32)
    part[...] = total.reshape(SPACE, SLICE, 2 * NEV)

    loads[3].wait()
    pl.semaphore_wait(barrier, len(peers))
    copies = []

    def send(src, dst, send_sem, recv_sem, device):
        copy = pltpu.make_async_remote_copy(
            src_ref=src, dst_ref=dst, send_sem=send_sem, recv_sem=recv_sem,
            device_id=device, device_id_type=MESH,
        )
        copy.start()
        copies.append(copy)
        return copy

    scatter = []
    for d in range(1, SPACE):
        to = lax.rem(space + d, SPACE)
        scatter.append(send(part.at[to], rs.at[d], rs_send.at[d], rs_recv.at[d], (t, to)))

    got = {}

    def share(name, block, device):
        n = len(got)
        got[name] = send(block, block, f_send.at[n], f_recv.at[n], device)

    def z_block(dx, flip):
        hi = 1 - y_hi if flip else y_hi
        return fbuf.at[step(x, dx), hi, z, :, ROWS_Z]

    def y_block(dx):
        return fbuf.at[step(x, dx), y_hi, :, y_lo, ROWS_Y]

    def x_block(flip):
        hi = 1 - y_hi if flip else y_hi
        return fbuf.at[x, hi, :, :, ROWS_X]

    for d in (2, 1, -1):
        share(("z1", d, True), z_block(0, False), chip(d, True, 0, True))
        share(("z1", d, False), z_block(0, False), chip(d, False, 0, False))
        share(("y1", d), y_block(0), chip(d, False, 0, False))
    share(("z1", 0, True), z_block(0, False), chip(0, True, 0, True))
    share(("x1",), x_block(False), chip(0, True, 0, True))
    for d in SHIFTS:
        share(("x2", d, False), x_block(False), chip(d, False, 0, False))
    for name, flips in (("across", ACROSS), ("two", TWO)):
        share(("y2", name, 0), y_block(0), chip(0, flips[0], 0, flips[1]))
    swap = send(
        back_hbm.at[:, 1 - core], bbuf.at[:, core], swap_sem.at[0], swap_sem.at[1], partner
    )

    elem = part[space]
    for d in range(1, SPACE):
        scatter[d - 1].wait_recv()
        elem += rs[d]
    own = k_own * SPACE + space
    ebuf[own] = (elem * (1.0 / math.sqrt(3.0 * SITES_TOTAL))).astype(BF16)
    away = [
        (dx, flip_hi, dz, flip_lo)
        for dx in (0, *SHIFTS) for flip_hi in (False, True)
        for dz in (0, *SHIFTS) for flip_lo in (False, True)
    ]
    def hops(at):
        dx, flip_hi, dz, flip_lo = at
        return abs(dx) + abs(dz) + (1 if flip_lo else 2 * flip_hi)
    for at in sorted(away[1:], key=hops, reverse=True):
        pltpu.make_async_remote_copy(
            src_ref=ebuf.at[own], dst_ref=ebuf.at[own], send_sem=e_send.at[0],
            recv_sem=e_recv.at[k_own], device_id=chip(*at), device_id_type=MESH,
        ).start()

    got["x1",].wait_recv()
    for d in SHIFTS:
        share(("x2", d, True), x_block(True), chip(d, False, 0, False))
    for d in SHIFTS:
        got["y1", d].wait_recv()
        for name, flips in (("two", TWO), ("across", ACROSS), ("pair", PAIR)):
            share(("y2", name, d), y_block(-d), chip(0, flips[0], 0, flips[1]))
    for dx, flip in [(0, True)] + [(d, f) for d in SHIFTS for f in (False, True)]:
        got["z1", dx, flip].wait_recv()
        for d in (2, 1, -1):
            share(("z2", dx, flip, d), z_block(-dx, flip), chip(0, False, d, False))

    loads[4].wait()
    swap.wait_recv()
    for spin in range(NS):
        power = gam_ref[1, spin]
        cosine = jnp.where(power == 0, 1.0, 0.0) - jnp.where(power == 2, 1.0, 0.0)
        sine = jnp.where(power == 1, 1.0, 0.0) - jnp.where(power == 3, 1.0, 0.0)
        lanes = pl.ds(spin * NEV, NEV)

        def turn(k, carry):
            for u in range(2):
                back_re = bbuf[k, u, 0:64, lanes].astype(F32)
                back_im = bbuf[k, u, 64:128, lanes].astype(F32)
                bbuf[k, u, 0:64, lanes] = (cosine * back_re - sine * back_im).astype(BF16)
                bbuf[k, u, 64:128, lanes] = (sine * back_re + cosine * back_im).astype(BF16)
            return carry

        lax.fori_loop(0, NT // 2, turn, 0)

    acc = jnp.zeros((4 * 64, 2 * NSRC), F32)
    for dx in (0, *SHIFTS):
        for flip in (False, True):
            x_at, hi_at = step(x, -dx), 1 - y_hi if flip else y_hi
            k = x_at * 2 + hi_at
            here = dx == 0 and not flip
            rows = pl.ds(k * SPACE, SPACE)
            count = pl.ds(0, SPACE - 1) if here else pl.ds(0, SPACE)
            pltpu.make_async_copy(ebuf.at[count], ebuf.at[count], e_recv.at[k]).wait()
            if not here:
                if dx:
                    got["x2", dx, flip].wait_recv()
                if flip:
                    got["y2", "across", dx].wait_recv()
                    got["y2", "two", dx].wait_recv()
                else:
                    got["y2", "pair", dx].wait_recv()
                for d in SHIFTS:
                    got["z2", dx, flip, d].wait_recv()
            elem = ebuf[rows].reshape(NEV, 2 * NEV)
            for spin in range(NS):
                fwd_re = fbuf[x_at, hi_at, spin // 2, spin % 2]
                fwd_im = fbuf[x_at, hi_at, 2 + spin // 2, spin % 2]
                right = jnp.concatenate([
                    jnp.concatenate([fwd_re, fwd_im], axis=1),
                    jnp.concatenate([-fwd_im, fwd_re], axis=1),
                ], axis=0)
                gbuf[spin] = jnp.dot(elem, right, preferred_element_type=F32).astype(BF16)
            image = jnp.concatenate([gbuf[gam_ref[0, spin]] for spin in range(NS)], axis=0)
            left = bbuf[k].reshape(4 * 64, NS * NEV)
            acc += jnp.dot(left, image, preferred_element_type=F32)
    for u in range(2):
        top = acc[u * 128 : u * 128 + 64]
        low = acc[u * 128 + 64 : u * 128 + 128]
        fin[u, 0] = top[:, :NSRC] - low[:, NSRC:]
        fin[u, 1] = top[:, NSRC:] + low[:, :NSRC]
    last = send(fin.at[1 - core], finr, fin_sem.at[0], fin_sem.at[1], partner)
    last.wait_recv()
    out_ref[...] = fin[core] + finr[...]
    for copy in copies:
        copy.wait_send()
    sent = pl.ds(0, 63)
    pltpu.make_async_copy(ebuf.at[sent], ebuf.at[sent], e_send.at[0]).wait()


def on_device(eigvecs, momenta, gamma_table, forward, backward):
    eig = eigvecs[0].transpose(0, 2, 1, 3)
    fwd = forward.reshape(4, 2, NEV, NSRC)
    back = backward.reshape(NT // 2, 2, 128, NS * NEV)
    dma = pltpu.SemaphoreType.DMA
    out = pl.pallas_call(
        kernel,
        name="three_point",
        out_shape=pltpu.VMEM((2, 64, NSRC), F32),
        in_specs=[pl.BlockSpec(memory_space=pltpu.SMEM)] * 2
        + [pl.BlockSpec(memory_space=pl.ANY)] * 3,
        out_specs=pl.BlockSpec(memory_space=pltpu.VMEM),
        scratch_shapes=[
            pltpu.VMEM((2, COLORS, NEV, SITES), BF16),
            pltpu.VMEM((4, 2, 4, 2, NEV, NSRC), BF16),
            pltpu.VMEM((NT // 2, 2, 128, NS * NEV), BF16),
            pltpu.VMEM((SPACE, SLICE, 2 * NEV), F32),
            pltpu.VMEM((SPACE, SLICE, 2 * NEV), F32),
            pltpu.VMEM((64, SLICE, 2 * NEV), BF16),
            pltpu.VMEM((NS, NEV, 2 * NSRC), BF16),
            pltpu.VMEM((2, 2, 64, NSRC), F32),
            pltpu.VMEM((2, 64, NSRC), F32),
            dma((5,)), dma((2,)), dma((SPACE,)), dma((SPACE,)),
            dma((1,)), dma((8,)), dma((49,)), dma((49,)), dma((2,)),
        ],
        compiler_params=pltpu.CompilerParams(collective_id=0, has_side_effects=True),
    )(momenta, gamma_table, eig, fwd, back)
    return out[None, None] * (1.0 / math.sqrt(NT))


def solution(mesh):
    placed = (
        P("tins", None, None, None, "space"),
        P(),
        P(),
        P("tins", None, None, None),
        P("tins", None, None, "space", None),
    )
    return jax.shard_map(
        on_device,
        mesh=mesh,
        in_specs=placed,
        out_specs=P("tins", None, None, "space", None),
        check_vma=False,
    )
```

```python
import functools
import math

import jax
import jax.numpy as jnp
from jax import lax
from jax.experimental import pallas as pl
from jax.experimental.pallas import tpu as pltpu
from jax.sharding import PartitionSpec as P

MESH = pl.DeviceIdType.MESH
F32 = jnp.float32
BF16 = jnp.bfloat16
NEV, NS, COLORS, LS, NSRC, NT, SPACE = 128, 4, 3, 96, 128, 16, 8
SITES_TOTAL = 4096
SITES = SITES_TOTAL // SPACE
SLICE = NEV // SPACE
ROWS_X, ROWS_Y, ROWS_Z = pl.ds(0, 48), pl.ds(48, 64), pl.ds(112, 16)
SHIFTS = (1, -1, 2)


def site_phases(mom_ref, space):
    site = (space * SITES + lax.broadcasted_iota(jnp.int32, (1, SITES), 1)).astype(F32)
    line = jnp.floor((site + 0.5) * (1.0 / LS))
    coord_x = site - LS * line
    coord_z = jnp.floor((line + 0.5) * (1.0 / LS))
    coord_y = line - LS * coord_z
    m = [mom_ref[0, i].astype(F32) for i in range(3)]
    turns = m[0] * coord_x + m[1] * coord_y + m[2] * coord_z
    turns = turns - LS * jnp.floor((turns + 0.5) * (1.0 / LS))
    angle = (2.0 * math.pi / LS) * turns
    return jnp.cos(angle), -jnp.sin(angle)


def kernel(
    mom_ref, gam_ref, eig_hbm, fwd_hbm, back_hbm, out_ref,
    eig, fbuf, bbuf, part, rs, ebuf, gbuf, fin, finr,
    load_sem, swap_sem, rs_send, rs_recv, e_send, e_recv, e2_send, e2_recv, f_send, f_recv, fin_sem,
):
    t = lax.axis_index("tins")
    space = lax.axis_index("space")
    core = lax.rem(t, 2)
    x, y_hi = lax.div(t, 4), lax.rem(lax.div(t, 2), 2)
    z, y_lo = lax.div(space, 2), lax.rem(space, 2)
    k_own = lax.div(t, 2)
    partner = (t + 1 - 2 * core, space)

    def step(v, d):
        return lax.rem(v + (d + 4) % 4, 4) if d % 4 else v

    def chip(dx, flip_hi, dz, flip_lo):
        hi = 1 - y_hi if flip_hi else y_hi
        lo = 1 - y_lo if flip_lo else y_lo
        return (step(x, dx) * 4 + hi * 2 + core, step(z, dz) * 2 + lo)

    PAIR, ACROSS, TWO = (False, True), (True, True), (True, False)

    loads = [pltpu.make_async_copy(eig_hbm.at[:, c], eig.at[:, c], load_sem.at[c]) for c in range(COLORS)]
    loads += [
        pltpu.make_async_copy(fwd_hbm, fbuf.at[x, y_hi], load_sem.at[3]),
        pltpu.make_async_copy(back_hbm.at[:, core], bbuf.at[:, core], load_sem.at[4]),
    ]
    for load in loads:
        load.start()

    barrier = pltpu.get_barrier_semaphore()
    peers = [partner]
    peers += [(t, lax.rem(space + d, SPACE)) for d in range(1, SPACE)]
    peers += [chip(d, False, 0, False) for d in SHIFTS]
    peers += [chip(d, True, 0, True) for d in (0, *SHIFTS)]
    peers += [chip(0, True, 0, False)]
    for peer in peers:
        pl.semaphore_signal(barrier, inc=1, device_id=peer, device_id_type=MESH)

    phase_re, phase_im = site_phases(mom_ref, space)
    total = jnp.zeros((NEV, 2 * NEV), F32)
    nt = (((1,), (1,)), ((), ()))
    for color in range(COLORS):
        loads[color].wait()
        vec_re = eig[0, color]
        vec_im = eig[1, color]
        wide_re, wide_im = vec_re.astype(F32), vec_im.astype(F32)
        wave_re = (phase_re * wide_re - phase_im * wide_im).astype(BF16)
        wave_im = (phase_re * wide_im + phase_im * wide_re).astype(BF16)
        right = jnp.concatenate([wave_re, wave_im], axis=0)
        total += lax.dot_general(vec_re, right, nt, preferred_element_type=F32)
        right = jnp.concatenate([wave_im, -wave_re], axis=0)
        total += lax.dot_general(vec_im, right, nt, preferred_element_type=F32)
    part[...] = total.reshape(SPACE, SLICE, 2 * NEV)

    loads[3].wait()
    pl.semaphore_wait(barrier, len(peers))
    copies = []

    def send(src, dst, send_sem, recv_sem, device):
        copy = pltpu.make_async_remote_copy(
            src_ref=src, dst_ref=dst, send_sem=send_sem, recv_sem=recv_sem,
            device_id=device, device_id_type=MESH,
        )
        copy.start()
        copies.append(copy)
        return copy

    scatter = []
    for d in range(1, SPACE):
        to = lax.rem(space + d, SPACE)
        scatter.append(send(part.at[to], rs.at[d], rs_send.at[d], rs_recv.at[d], (t, to)))

    got = {}

    def share(name, block, device):
        n = sum(key[0] != "e2" for key in got)
        got[name] = send(block, block, f_send.at[n], f_recv.at[n], device)

    def z_block(dx, flip):
        hi = 1 - y_hi if flip else y_hi
        return fbuf.at[step(x, dx), hi, z, :, ROWS_Z]

    def y_block(dx):
        return fbuf.at[step(x, dx), y_hi, :, y_lo, ROWS_Y]

    def x_block(flip):
        hi = 1 - y_hi if flip else y_hi
        return fbuf.at[x, hi, :, :, ROWS_X]

    for d in (2, 1, -1):
        share(("z1", d, True), z_block(0, False), chip(d, True, 0, True))
        share(("z1", d, False), z_block(0, False), chip(d, False, 0, False))
        share(("y1", d), y_block(0), chip(d, False, 0, False))
    share(("z1", 0, True), z_block(0, False), chip(0, True, 0, True))
    share(("x1",), x_block(False), chip(0, True, 0, True))
    share(("y2", "across", 0), y_block(0), chip(0, True, 0, True))
    swap = send(
        back_hbm.at[:, 1 - core], bbuf.at[:, core], swap_sem.at[0], swap_sem.at[1], partner
    )

    elem = part[space]
    for d in range(1, SPACE):
        scatter[d - 1].wait_recv()
        elem += rs[d]
    ebuf[k_own, space] = (elem * (1.0 / math.sqrt(3.0 * SITES_TOTAL))).astype(BF16)
    own = ebuf.at[k_own, space]
    for dx in (2, 1, -1, 0):
        for flips in (TWO, ACROSS, PAIR, (False, False)):
            if dx or flips[0] or flips[1]:
                pltpu.make_async_remote_copy(
                    src_ref=own, dst_ref=own, send_sem=e_send.at[0], recv_sem=e_recv.at[x],
                    device_id=chip(dx, flips[0], 0, flips[1]), device_id_type=MESH,
                ).start()

    for d in SHIFTS:
        share(("x2", d, False), x_block(False), chip(d, False, 0, False))
    got["x1",].wait_recv()
    for d in SHIFTS:
        share(("x2", d, True), x_block(True), chip(d, False, 0, False))
    for d in SHIFTS:
        got["y1", d].wait_recv()
        for name, flips in (("across", ACROSS), ("pair", PAIR)):
            share(("y2", name, d), y_block(-d), chip(0, flips[0], 0, flips[1]))
    for dx, flip in [(0, True)] + [(d, f) for d in SHIFTS for f in (False, True)]:
        got["z1", dx, flip].wait_recv()
        for d in (2, 1, -1):
            share(("z2", dx, flip, d), z_block(-dx, flip), chip(0, False, d, False))
    for i, dx in enumerate((0, *SHIFTS)):
        x_at = step(x, -dx)
        fill = ebuf.at[0, pl.ds(0, 3)] if dx == 0 else ebuf.at[pl.ds(0, 2), pl.ds(0, 2)]
        pltpu.make_async_copy(fill, fill, e_recv.at[x_at]).wait()
        four = ebuf.at[pl.ds(2 * x_at, 2), pl.ds(2 * z, 2)]
        for d in (2, 1, -1):
            got["e2", dx, d] = send(
                four, four, e2_send.at[i, d + 1], e2_recv.at[i, d + 1], chip(0, False, d, False)
            )
    for d in (0, *SHIFTS):
        got["y2", "across", d].wait_recv()
        passed = fbuf.at[step(x, -d), 1 - y_hi, :, 1 - y_lo, ROWS_Y]
        share(("y3", d), passed, chip(0, False, 0, True))

    loads[4].wait()
    swap.wait_recv()
    for spin in range(NS):
        power = gam_ref[1, spin]
        cosine = jnp.where(power == 0, 1.0, 0.0) - jnp.where(power == 2, 1.0, 0.0)
        sine = jnp.where(power == 1, 1.0, 0.0) - jnp.where(power == 3, 1.0, 0.0)
        lanes = pl.ds(spin * NEV, NEV)

        def turn(k, carry):
            for u in range(2):
                back_re = bbuf[k, u, 0:64, lanes].astype(F32)
                back_im = bbuf[k, u, 64:128, lanes].astype(F32)
                bbuf[k, u, 0:64, lanes] = (cosine * back_re - sine * back_im).astype(BF16)
                bbuf[k, u, 64:128, lanes] = (sine * back_re + cosine * back_im).astype(BF16)
            return carry

        lax.fori_loop(0, NT // 2, turn, 0)

    acc = jnp.zeros((4 * 64, 2 * NSRC), F32)
    for dx in (0, *SHIFTS):
        for flip in (False, True):
            x_at, hi_at = step(x, -dx), 1 - y_hi if flip else y_hi
            k = x_at * 2 + hi_at
            here = dx == 0 and not flip
            if not flip:
                for d in SHIFTS:
                    got["e2", dx, d].wait_recv()
            if not here:
                if dx:
                    got["x2", dx, flip].wait_recv()
                if flip:
                    got["y3", dx].wait_recv()
                else:
                    got["y2", "pair", dx].wait_recv()
                for d in SHIFTS:
                    got["z2", dx, flip, d].wait_recv()
            elem = ebuf[k].reshape(NEV, 2 * NEV)
            for spin in range(NS):
                fwd_re = fbuf[x_at, hi_at, spin // 2, spin % 2]
                fwd_im = fbuf[x_at, hi_at, 2 + spin // 2, spin % 2]
                right = jnp.concatenate([
                    jnp.concatenate([fwd_re, fwd_im], axis=1),
                    jnp.concatenate([-fwd_im, fwd_re], axis=1),
                ], axis=0)
                gbuf[spin] = jnp.dot(elem, right, preferred_element_type=F32).astype(BF16)
            image = jnp.concatenate([gbuf[gam_ref[0, spin]] for spin in range(NS)], axis=0)
            left = bbuf[k].reshape(4 * 64, NS * NEV)
            acc += jnp.dot(left, image, preferred_element_type=F32)
    for u in range(2):
        top = acc[u * 128 : u * 128 + 64]
        low = acc[u * 128 + 64 : u * 128 + 128]
        fin[u, 0] = top[:, :NSRC] - low[:, NSRC:]
        fin[u, 1] = top[:, NSRC:] + low[:, :NSRC]
    last = send(fin.at[1 - core], finr, fin_sem.at[0], fin_sem.at[1], partner)
    last.wait_recv()
    out_ref[...] = fin[core] + finr[...]
    for copy in copies:
        copy.wait_send()
    sent = ebuf.at[pl.ds(0, 3), pl.ds(0, 5)]
    pltpu.make_async_copy(sent, sent, e_send.at[0]).wait()


def on_device(eigvecs, momenta, gamma_table, forward, backward):
    eig = eigvecs[0].transpose(0, 2, 1, 3)
    fwd = forward.reshape(4, 2, NEV, NSRC)
    back = backward.reshape(NT // 2, 2, 128, NS * NEV)
    dma = pltpu.SemaphoreType.DMA
    out = pl.pallas_call(
        kernel,
        name="three_point",
        out_shape=pltpu.VMEM((2, 64, NSRC), F32),
        in_specs=[pl.BlockSpec(memory_space=pltpu.SMEM)] * 2
        + [pl.BlockSpec(memory_space=pl.ANY)] * 3,
        out_specs=pl.BlockSpec(memory_space=pltpu.VMEM),
        scratch_shapes=[
            pltpu.VMEM((2, COLORS, NEV, SITES), BF16),
            pltpu.VMEM((4, 2, 4, 2, NEV, NSRC), BF16),
            pltpu.VMEM((NT // 2, 2, 128, NS * NEV), BF16),
            pltpu.VMEM((SPACE, SLICE, 2 * NEV), F32),
            pltpu.VMEM((SPACE, SLICE, 2 * NEV), F32),
            pltpu.VMEM((NT // 2, SPACE, SLICE, 2 * NEV), BF16),
            pltpu.VMEM((NS, NEV, 2 * NSRC), BF16),
            pltpu.VMEM((2, 2, 64, NSRC), F32),
            pltpu.VMEM((2, 64, NSRC), F32),
            dma((5,)), dma((2,)), dma((SPACE,)), dma((SPACE,)),
            dma((1,)), dma((4,)), dma((4, 4)), dma((4, 4)), dma((49,)), dma((49,)), dma((2,)),
        ],
        compiler_params=pltpu.CompilerParams(collective_id=0, has_side_effects=True),
    )(momenta, gamma_table, eig, fwd, back)
    return out[None, None] * (1.0 / math.sqrt(NT))


def solution(mesh):
    placed = (
        P("tins", None, None, None, "space"),
        P(),
        P(),
        P("tins", None, None, None),
        P("tins", None, None, "space", None),
    )
    return jax.shard_map(
        on_device,
        mesh=mesh,
        in_specs=placed,
        out_specs=P("tins", None, None, "space", None),
        check_vma=False,
    )
```

```python
import functools
import math

import jax
import jax.numpy as jnp
from jax import lax
from jax.experimental import pallas as pl
from jax.experimental.pallas import tpu as pltpu
from jax.sharding import PartitionSpec as P

MESH = pl.DeviceIdType.MESH
F32 = jnp.float32
BF16 = jnp.bfloat16
NEV, NS, COLORS, LS, NSRC, NT, SPACE = 128, 4, 3, 96, 128, 16, 8
SITES_TOTAL = 4096
SITES = SITES_TOTAL // SPACE
SLICE = NEV // SPACE
ROWS_X, ROWS_Y, ROWS_Z = pl.ds(0, 48), pl.ds(48, 64), pl.ds(112, 16)
SHIFTS = (1, -1, 2)


def site_phases(mom_ref, space):
    site = (space * SITES + lax.broadcasted_iota(jnp.int32, (1, SITES), 1)).astype(F32)
    line = jnp.floor((site + 0.5) * (1.0 / LS))
    coord_x = site - LS * line
    coord_z = jnp.floor((line + 0.5) * (1.0 / LS))
    coord_y = line - LS * coord_z
    m = [mom_ref[0, i].astype(F32) for i in range(3)]
    turns = m[0] * coord_x + m[1] * coord_y + m[2] * coord_z
    turns = turns - LS * jnp.floor((turns + 0.5) * (1.0 / LS))
    angle = (2.0 * math.pi / LS) * turns
    return jnp.cos(angle), -jnp.sin(angle)


def kernel(
    mom_ref, gam_ref, eig_hbm, fwd_hbm, back_hbm, out_ref,
    eig, fbuf, bbuf, part, rs, ebuf, gbuf, fin, finr,
    load_sem, swap_sem, rs_send, rs_recv, e_send, e_recv, e2_send, e2_recv, f_send, f_recv, fin_sem,
):
    t = lax.axis_index("tins")
    space = lax.axis_index("space")
    core = lax.rem(t, 2)
    x, y_hi = lax.div(t, 4), lax.rem(lax.div(t, 2), 2)
    z, y_lo = lax.div(space, 2), lax.rem(space, 2)
    k_own = lax.div(t, 2)
    partner = (t + 1 - 2 * core, space)

    def step(v, d):
        return lax.rem(v + (d + 4) % 4, 4) if d % 4 else v

    def chip(dx, flip_hi, dz, flip_lo):
        hi = 1 - y_hi if flip_hi else y_hi
        lo = 1 - y_lo if flip_lo else y_lo
        return (step(x, dx) * 4 + hi * 2 + core, step(z, dz) * 2 + lo)

    PAIR, ACROSS, TWO = (False, True), (True, True), (True, False)

    barrier = pltpu.get_barrier_semaphore()
    shared = [(2, True), (2, False), (1, True), (-1, True), (1, False), (-1, False), (0, True)]
    peers = [chip(0, False, *at) for at in shared[:4]]
    peers += [chip(d, True, 0, True) for d in (2, 1, -1)]
    peers += [chip(0, False, *at) for at in shared[4:6]]
    peers += [chip(d, False, 0, False) for d in (2, 1, -1)]
    peers += [chip(0, *flips) for flips in ((True, 0, False), (True, 0, True), (False, 0, True))]
    peers += [partner]
    for peer in peers:
        pl.semaphore_signal(barrier, inc=1, device_id=peer, device_id_type=MESH)

    loads = [pltpu.make_async_copy(eig_hbm.at[:, c], eig.at[:, c], load_sem.at[c]) for c in range(COLORS)]
    loads += [
        pltpu.make_async_copy(fwd_hbm, fbuf.at[x, y_hi], load_sem.at[3]),
        pltpu.make_async_copy(back_hbm.at[:, core], bbuf.at[:, core], load_sem.at[4]),
    ]
    for load in loads:
        load.start()

    phase_re, phase_im = site_phases(mom_ref, space)
    total = jnp.zeros((NEV, 2 * NEV), F32)
    nt = (((1,), (1,)), ((), ()))
    for color in range(COLORS):
        loads[color].wait()
        vec_re = eig[0, color]
        vec_im = eig[1, color]
        wide_re, wide_im = vec_re.astype(F32), vec_im.astype(F32)
        wave_re = (phase_re * wide_re - phase_im * wide_im).astype(BF16)
        wave_im = (phase_re * wide_im + phase_im * wide_re).astype(BF16)
        right = jnp.concatenate([wave_re, wave_im], axis=0)
        total += lax.dot_general(vec_re, right, nt, preferred_element_type=F32)
        right = jnp.concatenate([wave_im, -wave_re], axis=0)
        total += lax.dot_general(vec_im, right, nt, preferred_element_type=F32)
    part[...] = total.reshape(SPACE, SLICE, 2 * NEV)

    loads[3].wait()
    pl.semaphore_wait(barrier, len(peers))
    copies = []

    def send(src, dst, send_sem, recv_sem, device):
        copy = pltpu.make_async_remote_copy(
            src_ref=src, dst_ref=dst, send_sem=send_sem, recv_sem=recv_sem,
            device_id=device, device_id_type=MESH,
        )
        copy.start()
        copies.append(copy)
        return copy

    scatter = []
    for d, at in enumerate(shared):
        to = chip(0, False, *at)
        scatter.append(send(part.at[to[1]], rs.at[d], rs_send.at[d], rs_recv.at[d], to))

    got = {}

    def share(name, block, device):
        n = sum(key[0] != "e2" for key in got)
        got[name] = send(block, block, f_send.at[n], f_recv.at[n], device)

    def z_block(dx, flip):
        hi = 1 - y_hi if flip else y_hi
        return fbuf.at[step(x, dx), hi, z, :, ROWS_Z]

    def y_block(dx):
        return fbuf.at[step(x, dx), y_hi, :, y_lo, ROWS_Y]

    def x_block(flip):
        hi = 1 - y_hi if flip else y_hi
        return fbuf.at[x, hi, :, :, ROWS_X]

    for d in (2, 1, -1):
        share(("z1", d, True), z_block(0, False), chip(d, True, 0, True))
        share(("z1", d, False), z_block(0, False), chip(d, False, 0, False))
        share(("y1", d), y_block(0), chip(d, False, 0, False))
    share(("z1", 0, True), z_block(0, False), chip(0, True, 0, True))
    share(("x1",), x_block(False), chip(0, True, 0, True))
    share(("y2", "across", 0), y_block(0), chip(0, True, 0, True))
    for d in (1, -1):
        share(("x2", d, False), x_block(False), chip(d, False, 0, False))
    swap = send(
        back_hbm.at[:, 1 - core], bbuf.at[:, core], swap_sem.at[0], swap_sem.at[1], partner
    )

    elem = part[space]
    for d in range(len(shared)):
        scatter[d].wait_recv()
        elem += rs[d]
    ebuf[k_own, space] = (elem * (1.0 / math.sqrt(3.0 * SITES_TOTAL))).astype(BF16)
    own = ebuf.at[k_own, space]
    for dx in (2, 1, -1, 0):
        for flips in (TWO, ACROSS, PAIR, (False, False)):
            if dx or flips[0] or flips[1]:
                pltpu.make_async_remote_copy(
                    src_ref=own, dst_ref=own, send_sem=e_send.at[0], recv_sem=e_recv.at[x],
                    device_id=chip(dx, flips[0], 0, flips[1]), device_id_type=MESH,
                ).start()

    for d in (2,):
        share(("x2", d, False), x_block(False), chip(d, False, 0, False))
    got["x1",].wait_recv()
    for d in SHIFTS:
        share(("x2", d, True), x_block(True), chip(d, False, 0, False))
    for d in SHIFTS:
        got["y1", d].wait_recv()
        for name, flips in (("across", ACROSS), ("pair", PAIR)):
            share(("y2", name, d), y_block(-d), chip(0, flips[0], 0, flips[1]))
    for dx, flip in [(0, True)] + [(d, f) for d in SHIFTS for f in (False, True)]:
        got["z1", dx, flip].wait_recv()
        for d in (2, 1, -1):
            share(("z2", dx, flip, d), z_block(-dx, flip), chip(0, False, d, False))
    for i, dx in enumerate((0, *SHIFTS)):
        x_at = step(x, -dx)
        fill = ebuf.at[0, pl.ds(0, 3)] if dx == 0 else ebuf.at[pl.ds(0, 2), pl.ds(0, 2)]
        pltpu.make_async_copy(fill, fill, e_recv.at[x_at]).wait()
        four = ebuf.at[pl.ds(2 * x_at, 2), pl.ds(2 * z, 2)]
        for d in SHIFTS:
            got["e2", dx, d] = send(
                four, four, e2_send.at[i, d + 1], e2_recv.at[i, d + 1], chip(0, False, d, False)
            )
    for d in (0, *SHIFTS):
        got["y2", "across", d].wait_recv()
        passed = fbuf.at[step(x, -d), 1 - y_hi, :, 1 - y_lo, ROWS_Y]
        share(("y3", d), passed, chip(0, False, 0, True))

    loads[4].wait()
    swap.wait_recv()
    for spin in range(NS):
        power = gam_ref[1, spin]
        cosine = jnp.where(power == 0, 1.0, 0.0) - jnp.where(power == 2, 1.0, 0.0)
        sine = jnp.where(power == 1, 1.0, 0.0) - jnp.where(power == 3, 1.0, 0.0)
        lanes = pl.ds(spin * NEV, NEV)

        def turn(k, carry):
            for u in range(2):
                back_re = bbuf[k, u, 0:64, lanes].astype(F32)
                back_im = bbuf[k, u, 64:128, lanes].astype(F32)
                bbuf[k, u, 0:64, lanes] = (cosine * back_re - sine * back_im).astype(BF16)
                bbuf[k, u, 64:128, lanes] = (sine * back_re + cosine * back_im).astype(BF16)
            return carry

        lax.fori_loop(0, NT // 2, turn, 0)

    acc = jnp.zeros((4 * 64, 2 * NSRC), F32)
    for dx in (0, *SHIFTS):
        for flip in (False, True):
            x_at, hi_at = step(x, -dx), 1 - y_hi if flip else y_hi
            k = x_at * 2 + hi_at
            here = dx == 0 and not flip
            if not flip:
                for d in SHIFTS:
                    got["e2", dx, d].wait_recv()
            if not here:
                if dx:
                    got["x2", dx, flip].wait_recv()
                if flip:
                    got["y3", dx].wait_recv()
                else:
                    got["y2", "pair", dx].wait_recv()
                for d in SHIFTS:
                    got["z2", dx, flip, d].wait_recv()
            elem = ebuf[k].reshape(NEV, 2 * NEV)
            for spin in range(NS):
                fwd_re = fbuf[x_at, hi_at, spin // 2, spin % 2]
                fwd_im = fbuf[x_at, hi_at, 2 + spin // 2, spin % 2]
                right = jnp.concatenate([
                    jnp.concatenate([fwd_re, fwd_im], axis=1),
                    jnp.concatenate([-fwd_im, fwd_re], axis=1),
                ], axis=0)
                gbuf[spin] = jnp.dot(elem, right, preferred_element_type=F32).astype(BF16)
            image = jnp.concatenate([gbuf[gam_ref[0, spin]] for spin in range(NS)], axis=0)
            left = bbuf[k].reshape(4 * 64, NS * NEV)
            acc += jnp.dot(left, image, preferred_element_type=F32)
    for u in range(2):
        top = acc[u * 128 : u * 128 + 64]
        low = acc[u * 128 + 64 : u * 128 + 128]
        fin[u, 0] = top[:, :NSRC] - low[:, NSRC:]
        fin[u, 1] = top[:, NSRC:] + low[:, :NSRC]
    last = send(fin.at[1 - core], finr, fin_sem.at[0], fin_sem.at[1], partner)
    last.wait_recv()
    out_ref[...] = fin[core] + finr[...]
    for copy in copies:
        copy.wait_send()
    sent = ebuf.at[pl.ds(0, 3), pl.ds(0, 5)]
    pltpu.make_async_copy(sent, sent, e_send.at[0]).wait()


def on_device(eigvecs, momenta, gamma_table, forward, backward):
    eig = eigvecs[0].transpose(0, 2, 1, 3)
    fwd = forward.reshape(4, 2, NEV, NSRC)
    back = backward.reshape(NT // 2, 2, 128, NS * NEV)
    dma = pltpu.SemaphoreType.DMA
    out = pl.pallas_call(
        kernel,
        name="three_point",
        out_shape=pltpu.VMEM((2, 64, NSRC), F32),
        in_specs=[pl.BlockSpec(memory_space=pltpu.SMEM)] * 2
        + [pl.BlockSpec(memory_space=pl.ANY)] * 3,
        out_specs=pl.BlockSpec(memory_space=pltpu.VMEM),
        scratch_shapes=[
            pltpu.VMEM((2, COLORS, NEV, SITES), BF16),
            pltpu.VMEM((4, 2, 4, 2, NEV, NSRC), BF16),
            pltpu.VMEM((NT // 2, 2, 128, NS * NEV), BF16),
            pltpu.VMEM((SPACE, SLICE, 2 * NEV), F32),
            pltpu.VMEM((SPACE, SLICE, 2 * NEV), F32),
            pltpu.VMEM((NT // 2, SPACE, SLICE, 2 * NEV), BF16),
            pltpu.VMEM((NS, NEV, 2 * NSRC), BF16),
            pltpu.VMEM((2, 2, 64, NSRC), F32),
            pltpu.VMEM((2, 64, NSRC), F32),
            dma((5,)), dma((2,)), dma((SPACE,)), dma((SPACE,)),
            dma((1,)), dma((4,)), dma((4, 4)), dma((4, 4)), dma((49,)), dma((49,)), dma((2,)),
        ],
        compiler_params=pltpu.CompilerParams(collective_id=0, has_side_effects=True),
    )(momenta, gamma_table, eig, fwd, back)
    return out[None, None] * (1.0 / math.sqrt(NT))


def solution(mesh):
    placed = (
        P("tins", None, None, None, "space"),
        P(),
        P(),
        P("tins", None, None, None),
        P("tins", None, None, "space", None),
    )
    return jax.shard_map(
        on_device,
        mesh=mesh,
        in_specs=placed,
        out_specs=P("tins", None, None, "space", None),
        check_vma=False,
    )
```

```python
import functools
import math

import jax
import jax.numpy as jnp
from jax import lax
from jax.experimental import pallas as pl
from jax.experimental.pallas import tpu as pltpu
from jax.sharding import PartitionSpec as P

MESH = pl.DeviceIdType.MESH
F32 = jnp.float32
BF16 = jnp.bfloat16
NEV, NS, COLORS, LS, NSRC, NT, SPACE = 128, 4, 3, 96, 128, 16, 8
SITES_TOTAL = 4096
SITES = SITES_TOTAL // SPACE
SLICE = NEV // SPACE
ROWS_X, ROWS_Y, ROWS_Z = pl.ds(0, 48), pl.ds(48, 64), pl.ds(112, 16)
SHIFTS = (1, -1, 2)


def site_phases(mom_ref, space):
    site = (space * SITES + lax.broadcasted_iota(jnp.int32, (1, SITES), 1)).astype(F32)
    line = jnp.floor((site + 0.5) * (1.0 / LS))
    coord_x = site - LS * line
    coord_z = jnp.floor((line + 0.5) * (1.0 / LS))
    coord_y = line - LS * coord_z
    m = [mom_ref[0, i].astype(F32) for i in range(3)]
    turns = m[0] * coord_x + m[1] * coord_y + m[2] * coord_z
    turns = turns - LS * jnp.floor((turns + 0.5) * (1.0 / LS))
    angle = (2.0 * math.pi / LS) * turns
    return jnp.cos(angle), -jnp.sin(angle)


def kernel(
    mom_ref, gam_ref, eig_hbm, fwd_hbm, back_hbm, out_ref,
    eig, fbuf, bbuf, part, rs, ebuf, gbuf, fin, finr,
    load_sem, swap_sem, rs_send, rs_recv, e_send, e_recv, e2_send, e2_recv, f_send, f_recv, fin_sem,
):
    t = lax.axis_index("tins")
    space = lax.axis_index("space")
    core = lax.rem(t, 2)
    x, y_hi = lax.div(t, 4), lax.rem(lax.div(t, 2), 2)
    z, y_lo = lax.div(space, 2), lax.rem(space, 2)
    k_own = lax.div(t, 2)
    partner = (t + 1 - 2 * core, space)

    def step(v, d):
        return lax.rem(v + (d + 4) % 4, 4) if d % 4 else v

    def chip(dx, flip_hi, dz, flip_lo):
        hi = 1 - y_hi if flip_hi else y_hi
        lo = 1 - y_lo if flip_lo else y_lo
        return (step(x, dx) * 4 + hi * 2 + core, step(z, dz) * 2 + lo)

    PAIR, ACROSS, TWO = (False, True), (True, True), (True, False)

    barrier = pltpu.get_barrier_semaphore()
    shared = [(2, True), (2, False), (1, True), (-1, True), (1, False), (-1, False), (0, True)]
    peers = [chip(0, False, *at) for at in shared[:4]]
    peers += [chip(d, True, 0, True) for d in (2, 1, -1)]
    peers += [chip(0, False, *at) for at in shared[4:6]]
    peers += [chip(d, False, 0, False) for d in (2, 1, -1)]
    peers += [chip(0, *flips) for flips in ((True, 0, False), (True, 0, True), (False, 0, True))]
    peers += [partner]
    for peer in peers:
        pl.semaphore_signal(barrier, inc=1, device_id=peer, device_id_type=MESH)

    loads = [pltpu.make_async_copy(eig_hbm.at[:, c], eig.at[:, c], load_sem.at[c]) for c in range(COLORS)]
    loads += [
        pltpu.make_async_copy(fwd_hbm, fbuf.at[x, y_hi], load_sem.at[3]),
        pltpu.make_async_copy(back_hbm.at[:, core], bbuf.at[:, core], load_sem.at[4]),
    ]
    for load in loads:
        load.start()

    phase_re, phase_im = site_phases(mom_ref, space)
    total = jnp.zeros((NEV, 2 * NEV), F32)
    nt = (((1,), (1,)), ((), ()))
    for color in range(COLORS):
        loads[color].wait()
        vec_re = eig[0, color]
        vec_im = eig[1, color]
        wide_re, wide_im = vec_re.astype(F32), vec_im.astype(F32)
        wave_re = (phase_re * wide_re - phase_im * wide_im).astype(BF16)
        wave_im = (phase_re * wide_im + phase_im * wide_re).astype(BF16)
        right = jnp.concatenate([wave_re, wave_im], axis=0)
        total += lax.dot_general(vec_re, right, nt, preferred_element_type=F32)
        right = jnp.concatenate([wave_im, -wave_re], axis=0)
        total += lax.dot_general(vec_im, right, nt, preferred_element_type=F32)
    part[...] = total.reshape(SPACE, SLICE, 2 * NEV)

    loads[3].wait()
    pl.semaphore_wait(barrier, len(peers))
    copies = []

    def send(src, dst, send_sem, recv_sem, device):
        copy = pltpu.make_async_remote_copy(
            src_ref=src, dst_ref=dst, send_sem=send_sem, recv_sem=recv_sem,
            device_id=device, device_id_type=MESH,
        )
        copy.start()
        copies.append(copy)
        return copy

    scatter = []
    for d, at in enumerate(shared):
        to = chip(0, False, *at)
        scatter.append(send(part.at[to[1]], rs.at[d], rs_send.at[d], rs_recv.at[d], to))

    got = {}

    def share(name, block, device):
        n = sum(key[0] != "e2" for key in got)
        got[name] = send(block, block, f_send.at[n], f_recv.at[n], device)

    def z_block(dx, flip):
        hi = 1 - y_hi if flip else y_hi
        return fbuf.at[step(x, dx), hi, z, :, ROWS_Z]

    def y_block(dx):
        return fbuf.at[step(x, dx), y_hi, :, y_lo, ROWS_Y]

    def x_block(flip):
        hi = 1 - y_hi if flip else y_hi
        return fbuf.at[x, hi, :, :, ROWS_X]

    for d in (2, 1, -1):
        share(("z1", d, True), z_block(0, False), chip(d, True, 0, True))
        share(("z1", d, False), z_block(0, False), chip(d, False, 0, False))
        share(("y1", d), y_block(0), chip(d, False, 0, False))
    share(("z1", 0, True), z_block(0, False), chip(0, True, 0, True))
    share(("x1",), x_block(False), chip(0, True, 0, True))
    for d in (1, -1):
        share(("x2", d, False), x_block(False), chip(d, False, 0, False))
    swap = send(
        back_hbm.at[:, 1 - core], bbuf.at[:, core], swap_sem.at[0], swap_sem.at[1], partner
    )

    elem = part[space]
    for d in range(len(shared)):
        scatter[d].wait_recv()
        elem += rs[d]
    ebuf[k_own, space] = (elem * (1.0 / math.sqrt(3.0 * SITES_TOTAL))).astype(BF16)
    own = ebuf.at[k_own, space]
    for dx in (2, 1, -1, 0):
        for flips in (TWO, ACROSS, PAIR, (False, False)):
            if dx or flips[0] or flips[1]:
                pltpu.make_async_remote_copy(
                    src_ref=own, dst_ref=own, send_sem=e_send.at[0], recv_sem=e_recv.at[x],
                    device_id=chip(dx, flips[0], 0, flips[1]), device_id_type=MESH,
                ).start()

    share(("y2", "across", 0), y_block(0), chip(0, True, 0, True))
    got["x1",].wait_recv()
    for d in SHIFTS:
        share(("x2", d, True), x_block(True), chip(d, False, 0, False))
    for d in (2,):
        share(("x2", d, False), x_block(False), chip(d, False, 0, False))
    for d in SHIFTS:
        got["y1", d].wait_recv()
        for name, flips in (("across", ACROSS), ("pair", PAIR)):
            share(("y2", name, d), y_block(-d), chip(0, flips[0], 0, flips[1]))
    for dx, flip in [(0, True)] + [(d, f) for d in SHIFTS for f in (False, True)]:
        got["z1", dx, flip].wait_recv()
        for d in (2, 1, -1):
            share(("z2", dx, flip, d), z_block(-dx, flip), chip(0, False, d, False))
    for i, dx in enumerate((0, *SHIFTS)):
        x_at = step(x, -dx)
        fill = ebuf.at[0, pl.ds(0, 3)] if dx == 0 else ebuf.at[pl.ds(0, 2), pl.ds(0, 2)]
        pltpu.make_async_copy(fill, fill, e_recv.at[x_at]).wait()
        four = ebuf.at[pl.ds(2 * x_at, 2), pl.ds(2 * z, 2)]
        for d in SHIFTS:
            got["e2", dx, d] = send(
                four, four, e2_send.at[i, d + 1], e2_recv.at[i, d + 1], chip(0, False, d, False)
            )
    for d in (0, *SHIFTS):
        got["y2", "across", d].wait_recv()
        passed = fbuf.at[step(x, -d), 1 - y_hi, :, 1 - y_lo, ROWS_Y]
        share(("y3", d), passed, chip(0, False, 0, True))

    loads[4].wait()
    swap.wait_recv()
    for spin in range(NS):
        power = gam_ref[1, spin]
        cosine = jnp.where(power == 0, 1.0, 0.0) - jnp.where(power == 2, 1.0, 0.0)
        sine = jnp.where(power == 1, 1.0, 0.0) - jnp.where(power == 3, 1.0, 0.0)
        lanes = pl.ds(spin * NEV, NEV)

        def turn(k, carry):
            for u in range(2):
                back_re = bbuf[k, u, 0:64, lanes].astype(F32)
                back_im = bbuf[k, u, 64:128, lanes].astype(F32)
                bbuf[k, u, 0:64, lanes] = (cosine * back_re - sine * back_im).astype(BF16)
                bbuf[k, u, 64:128, lanes] = (sine * back_re + cosine * back_im).astype(BF16)
            return carry

        lax.fori_loop(0, NT // 2, turn, 0)

    acc = jnp.zeros((4 * 64, 2 * NSRC), F32)
    for dx in (0, *SHIFTS):
        for flip in (False, True):
            x_at, hi_at = step(x, -dx), 1 - y_hi if flip else y_hi
            k = x_at * 2 + hi_at
            here = dx == 0 and not flip
            if not flip:
                for d in SHIFTS:
                    got["e2", dx, d].wait_recv()
            if not here:
                if dx:
                    got["x2", dx, flip].wait_recv()
                if flip:
                    got["y3", dx].wait_recv()
                else:
                    got["y2", "pair", dx].wait_recv()
                for d in SHIFTS:
                    got["z2", dx, flip, d].wait_recv()
            elem = ebuf[k].reshape(NEV, 2 * NEV)
            for spin in range(NS):
                fwd_re = fbuf[x_at, hi_at, spin // 2, spin % 2]
                fwd_im = fbuf[x_at, hi_at, 2 + spin // 2, spin % 2]
                right = jnp.concatenate([
                    jnp.concatenate([fwd_re, fwd_im], axis=1),
                    jnp.concatenate([-fwd_im, fwd_re], axis=1),
                ], axis=0)
                gbuf[spin] = jnp.dot(elem, right, preferred_element_type=F32).astype(BF16)
            image = jnp.concatenate([gbuf[gam_ref[0, spin]] for spin in range(NS)], axis=0)
            left = bbuf[k].reshape(4 * 64, NS * NEV)
            acc += jnp.dot(left, image, preferred_element_type=F32)
    for u in range(2):
        top = acc[u * 128 : u * 128 + 64]
        low = acc[u * 128 + 64 : u * 128 + 128]
        fin[u, 0] = top[:, :NSRC] - low[:, NSRC:]
        fin[u, 1] = top[:, NSRC:] + low[:, :NSRC]
    last = send(fin.at[1 - core], finr, fin_sem.at[0], fin_sem.at[1], partner)
    last.wait_recv()
    out_ref[...] = fin[core] + finr[...]
    for copy in copies:
        copy.wait_send()
    sent = ebuf.at[pl.ds(0, 3), pl.ds(0, 5)]
    pltpu.make_async_copy(sent, sent, e_send.at[0]).wait()


def on_device(eigvecs, momenta, gamma_table, forward, backward):
    eig = eigvecs[0].transpose(0, 2, 1, 3)
    fwd = forward.reshape(4, 2, NEV, NSRC)
    back = backward.reshape(NT // 2, 2, 128, NS * NEV)
    dma = pltpu.SemaphoreType.DMA
    out = pl.pallas_call(
        kernel,
        name="three_point",
        out_shape=pltpu.VMEM((2, 64, NSRC), F32),
        in_specs=[pl.BlockSpec(memory_space=pltpu.SMEM)] * 2
        + [pl.BlockSpec(memory_space=pl.ANY)] * 3,
        out_specs=pl.BlockSpec(memory_space=pltpu.VMEM),
        scratch_shapes=[
            pltpu.VMEM((2, COLORS, NEV, SITES), BF16),
            pltpu.VMEM((4, 2, 4, 2, NEV, NSRC), BF16),
            pltpu.VMEM((NT // 2, 2, 128, NS * NEV), BF16),
            pltpu.VMEM((SPACE, SLICE, 2 * NEV), F32),
            pltpu.VMEM((SPACE, SLICE, 2 * NEV), F32),
            pltpu.VMEM((NT // 2, SPACE, SLICE, 2 * NEV), BF16),
            pltpu.VMEM((NS, NEV, 2 * NSRC), BF16),
            pltpu.VMEM((2, 2, 64, NSRC), F32),
            pltpu.VMEM((2, 64, NSRC), F32),
            dma((5,)), dma((2,)), dma((SPACE,)), dma((SPACE,)),
            dma((1,)), dma((4,)), dma((4, 4)), dma((4, 4)), dma((49,)), dma((49,)), dma((2,)),
        ],
        compiler_params=pltpu.CompilerParams(collective_id=0, has_side_effects=True),
    )(momenta, gamma_table, eig, fwd, back)
    return out[None, None] * (1.0 / math.sqrt(NT))


def solution(mesh):
    placed = (
        P("tins", None, None, None, "space"),
        P(),
        P(),
        P("tins", None, None, None),
        P("tins", None, None, "space", None),
    )
    return jax.shard_map(
        on_device,
        mesh=mesh,
        in_specs=placed,
        out_specs=P("tins", None, None, "space", None),
        check_vma=False,
    )
```
